512 devices in a mesh: dp: 32 (over z, core), fsdp: 16 (over x, y).
Axes of the slice: x: 4, y: 4, z: 16, core: 2. Of those that a mesh axis runs over, the one named last changes fastest.
Arguments:
- gradients: bfloat16 [1, 8192, 28672], P(None, 'fsdp', 'dp'), may hold values from -16 to 16
- errors: bfloat16 [1, 8192, 28672], P(None, 'fsdp', 'dp'), may hold values from -4 to 4
- start_factor: float32 [1, 32, 28672], P(None, None, 'dp'), may hold values from -6 to 6
Outputs:
- compressed: bfloat16 [1, 8192, 28672], P(None, 'fsdp', 'dp')
- new_errors: bfloat16 [1, 8192, 28672], P(None, 'fsdp', 'dp')
The draws below stay inside these ranges and needn't reach their ends.
All inputs are finite; a program needn't handle non-finite values.
Results may differ from the reference program's by a relative error of at most 0.0085.
Values sent between devices are 32-bit elements; how exact they have to be, the bound alone decides.
No kernel may reach another device: no remote copies, remote signals or barrier semaphores. Data moves between devices by JAX's collectives and lax.ppermute only.
A program may use at most 64 MiB of HBM per device.

```python
import math
import jax
import jax.numpy as jnp
from jax import lax

MATS = 1
D = 8192
C = 28672
RANK = 32


def draw_gradients(key, part):
    keys = jax.random.split(key, 7)
    components = 2 * RANK
    left = jax.random.normal(keys[0], (MATS, D, components), jnp.float32)
    right = jax.random.normal(keys[1], (MATS, components, C), jnp.float32)
    strength = jnp.exp(jax.random.uniform(keys[2], (MATS, components), jnp.float32, math.log(0.5), 0.0))
    lowrank = jnp.einsum('mdk,mkc->mdc', left * strength[:, None, :], right) / math.sqrt(components)
    position = jnp.arange(D, dtype=jnp.float32) / max(D - 1, 1)
    row_scale = (0.5 + position)[None, :] * jnp.exp(jax.random.uniform(keys[3], (MATS, D), jnp.float32, -0.7, 0.7))
    col_pos = jnp.arange(C, dtype=jnp.float32) / max(C - 1, 1)
    col_scale = (1.0 + 2.0 * col_pos)[None, :] * jnp.exp(jax.random.uniform(keys[4], (MATS, C), jnp.float32, -0.7, 0.7))
    noise = jax.random.normal(keys[6], (MATS, D, C), jnp.float32)
    values = lowrank + noise
    values = values * row_scale[:, :, None] * col_scale[:, None, :]
    return jnp.clip(values, -16.0, 16.0).astype(jnp.bfloat16)


def level_of(rng, extent, pieces, low, high):
    def one(dim, parts):
        steps = jax.random.uniform(jax.random.fold_in(jax.random.fold_in(rng, 6), dim), (parts,), jnp.float32, low / len(pieces), high / len(pieces))
        return jnp.repeat(jnp.exp(steps), extent[dim] // parts).reshape((-1,) + (1,) * (len(extent) - dim - 1))

    factor_of = one(*pieces[0])
    for cut in pieces[1:]:
        factor_of = factor_of * one(*cut)
    return factor_of


def gaussian(stream_key, extent, spread, reach, cuts=(), kind=jnp.bfloat16):
    values = jax.random.normal(stream_key, extent, jnp.float32) * spread
    if len(cuts) > 0:
        values = level_of(stream_key, extent, cuts, -0.22, 0.18) * values
    return jnp.clip(values, min=-reach, max=reach).astype(kind)


def setup_inputs(seed: int = 0) -> dict:
    seeds = jax.random.split(jax.random.key(seed), 4)
    return {
        "gradients": draw_gradients(jax.random.fold_in(seeds[3], 71), 0),
        "errors": gaussian(seeds[1], (MATS, D, C), 0.5, 4.0, ((1, 16), (2, 32))),
        "start_factor": gaussian(seeds[2], (MATS, RANK, C), 1.0, 6.0, ((2, 32),), jnp.float32),
    }


def reference(gradients, errors, start_factor):
    compressed_list = []
    error_list = []
    for matrix in range(MATS):
        combined = (gradients[matrix].astype(jnp.float32) + errors[matrix].astype(jnp.float32)).astype(jnp.bfloat16)
        factor_low = start_factor[matrix].astype(jnp.bfloat16)
        p_sum = jnp.dot(factor_low.astype(jnp.float32), combined.T.astype(jnp.float32), preferred_element_type=jnp.float32)
        gram = jnp.dot(p_sum.astype(jnp.float32), p_sum.T.astype(jnp.float32), precision=lax.Precision.HIGHEST, preferred_element_type=jnp.float32)
        lower = jnp.linalg.cholesky(gram)
        basis = jax.scipy.linalg.solve_triangular(lower, p_sum, lower=True)
        basis_low = basis.astype(jnp.bfloat16)
        factor_new = jnp.dot(basis_low.astype(jnp.float32), combined.astype(jnp.float32), preferred_element_type=jnp.float32)
        rebuilt = jnp.dot(basis.T.astype(jnp.float32), factor_new.astype(jnp.float32), precision=lax.Precision.HIGHEST, preferred_element_type=jnp.float32)
        compressed_list.append(rebuilt.astype(jnp.bfloat16))
        error_list.append((combined.astype(jnp.float32) - rebuilt).astype(jnp.bfloat16))
    return (jnp.stack(compressed_list), jnp.stack(error_list))
```

```python
import functools

import jax
import jax.numpy as jnp
from jax import lax
from jax.experimental import pallas as pl
from jax.experimental.pallas import tpu as pltpu
from jax.sharding import PartitionSpec as P

F32 = jnp.float32
BF16 = jnp.bfloat16
RANK = 32
VMEM = pltpu.VMEM


def split3(x):
    a = x.astype(BF16)
    r = x - a.astype(F32)
    b = r.astype(BF16)
    c = (r - b.astype(F32)).astype(BF16)
    return a, b, c


def first_kernel(g_ref, e_ref, s_ref, c_ref, part_ref):
    c = (g_ref[...].astype(F32) + e_ref[...].astype(F32)).astype(BF16)
    c_ref[...] = c
    q = s_ref[...].astype(BF16)
    part_ref[0] = lax.dot_general(q, c, (((1,), (1,)), ((), ())), preferred_element_type=F32)


def first(g, e, s, parts):
    rows, cols = g.shape
    step = rows // parts
    return pl.pallas_call(
        first_kernel,
        grid=(parts,),
        in_specs=[
            pl.BlockSpec((step, cols), lambda i: (i, 0)),
            pl.BlockSpec((step, cols), lambda i: (i, 0)),
            pl.BlockSpec((RANK, cols), lambda i: (0, 0)),
        ],
        out_specs=[
            pl.BlockSpec((step, cols), lambda i: (i, 0)),
            pl.BlockSpec((1, RANK, step), lambda i: (i, 0, 0)),
        ],
        out_shape=[
            jax.ShapeDtypeStruct((rows, cols), BF16),
            jax.ShapeDtypeStruct((parts, RANK, step), F32),
        ],
        compiler_params=pltpu.CompilerParams(vmem_limit_bytes=16 << 20),
        name="first",
    )(g, e, s)


def sum_kernel(copies, x_ref, o_ref):
    total = x_ref[0]
    for k in range(1, x_ref.shape[0]):
        total = total + x_ref[k]
    for k in range(copies):
        o_ref[k] = total


def sum_copies(x, copies):
    return pl.pallas_call(
        functools.partial(sum_kernel, copies),
        out_shape=jax.ShapeDtypeStruct((copies,) + x.shape[1:], F32),
        compiler_params=pltpu.CompilerParams(vmem_limit_bytes=16 << 20),
        name="sum_copies",
    )(x)


def product_kernel(copies, p_ref, c_ref, o_ref):
    parts = p_ref.shape[0]
    terms = [split3(p_ref[k]) for k in range(parts)]
    left = jnp.concatenate([jnp.concatenate([t[j] for t in terms], axis=1) for j in range(3)], axis=0)
    t3 = jnp.dot(left, c_ref[...], preferred_element_type=F32)
    t = t3[:RANK] + t3[RANK : 2 * RANK] + t3[2 * RANK :]
    g3 = lax.dot_general(left, left, (((1,), (1,)), ((), ())), preferred_element_type=F32)
    gr = g3[:RANK] + g3[RANK : 2 * RANK] + g3[2 * RANK :]
    gram = gr[:, :RANK] + gr[:, RANK : 2 * RANK] + gr[:, 2 * RANK : 3 * RANK]
    packed = jnp.concatenate([gram[8 * k : 8 * k + 8] for k in range(4)], axis=1)
    chunks = c_ref.shape[1] // 128
    for k in range(copies):
        for j in range(chunks):
            o_ref[k, j * RANK : (j + 1) * RANK] = t[:, j * 128 : (j + 1) * 128]
        o_ref[k, chunks * RANK : chunks * RANK + 8] = packed


def product(p, c, copies):
    chunks = c.shape[1] // 128
    return pl.pallas_call(
        functools.partial(product_kernel, copies),
        out_shape=jax.ShapeDtypeStruct((copies, chunks * RANK + 8, 128), F32),
        compiler_params=pltpu.CompilerParams(vmem_limit_bytes=16 << 20),
        name="product",
    )(p, c)


def inverse_factor(gram):
    rows = lax.broadcasted_iota(jnp.int32, (RANK, RANK), 0)
    cols = lax.broadcasted_iota(jnp.int32, (RANK, RANK), 1)
    w = jnp.concatenate([gram, (rows == cols).astype(F32)], axis=1)
    below = lax.broadcasted_iota(jnp.int32, (RANK, 1), 0)
    scale = jnp.zeros((RANK, 1), F32)
    for k in range(RANK):
        row = w[k : k + 1]
        inv = 1.0 / row[:, k : k + 1]
        col = jnp.where(below > k, w[:, k : k + 1], 0.0)
        scale = jnp.where(below == k, inv, scale)
        w = w - col * (row * inv)
    return w[:, RANK:] * jnp.sqrt(scale)


def last_kernel(x_ref, p_ref, c_ref, comp_ref, err_ref):
    parts, _, step = p_ref.shape
    chunks = c_ref.shape[1] // 128
    total = x_ref[0]
    for k in range(1, x_ref.shape[0]):
        total = total + x_ref[k]
    t = jnp.concatenate([total[j * RANK : (j + 1) * RANK] for j in range(chunks)], axis=1)
    packed = total[chunks * RANK :]
    gram = jnp.concatenate([packed[:, RANK * k : RANK * (k + 1)] for k in range(4)], axis=0)
    low = inverse_factor(gram)
    f = jnp.dot(low, t, precision=lax.Precision.HIGHEST, preferred_element_type=F32)
    z = lax.dot_general(low, f, (((0,), (0,)), ((), ())), precision=lax.Precision.HIGHEST, preferred_element_type=F32)
    z1, z2, _ = split3(z)
    right = jnp.concatenate([z1, z2, z1], axis=0)
    for k in range(parts):
        p1, p2, _ = split3(p_ref[k])
        left = jnp.concatenate([p1, p1, p2], axis=0)
        rebuilt = lax.dot_general(left, right, (((0,), (0,)), ((), ())), preferred_element_type=F32)
        at = pl.ds(k * step, step)
        comp_ref[at] = rebuilt.astype(BF16)
        err_ref[at] = (c_ref[at].astype(F32) - rebuilt).astype(BF16)


def last(x, p, c):
    return pl.pallas_call(
        last_kernel,
        out_shape=[jax.ShapeDtypeStruct(c.shape, BF16)] * 2,
        compiler_params=pltpu.CompilerParams(vmem_limit_bytes=24 << 20),
        name="last",
    )(x, p, c)


def groups(size, key):
    table = {}
    for i in range(size):
        table.setdefault(key(i), []).append(i)
    return list(table.values())


def shards(near, far, y_groups, x_groups, gradients, errors, start_factor):
    def exchange(x, axis, members):
        return lax.all_to_all(x, axis, 0, 0, tiled=True, axis_index_groups=members)

    parts = len(near[0])
    c, part = first(gradients[0], errors[0], start_factor[0], parts)
    part = exchange(part, "dp", near)
    piece = sum_copies(part, len(far[0]))
    piece = exchange(piece, "dp", far)
    piece = sum_copies(piece, parts)
    p = exchange(piece, "dp", near)
    t = product(p, c, len(y_groups[0]))
    t = exchange(t, "fsdp", y_groups)
    t = sum_copies(t, len(x_groups[0]))
    t = exchange(t, "fsdp", x_groups)
    compressed, new_errors = last(t, p, c)
    return compressed[None], new_errors[None]


def solution(mesh):
    dp, fsdp = mesh.shape["dp"], mesh.shape["fsdp"]
    body = functools.partial(
        shards,
        groups(dp, lambda i: i // 4),
        groups(dp, lambda i: i % 4),
        groups(fsdp, lambda i: i // 4),
        groups(fsdp, lambda i: i % 4),
    )
    return jax.shard_map(
        body,
        mesh=mesh,
        in_specs=(P(None, "fsdp", "dp"), P(None, "fsdp", "dp"), P(None, None, "dp")),
        out_specs=(P(None, "fsdp", "dp"), P(None, "fsdp", "dp")),
        check_vma=False,
    )
```

```python
import functools

import jax
import jax.numpy as jnp
from jax import lax
from jax.experimental import pallas as pl
from jax.experimental.pallas import tpu as pltpu
from jax.sharding import PartitionSpec as P

F32 = jnp.float32
BF16 = jnp.bfloat16
RANK = 32
VMEM = pltpu.VMEM


def split3(x):
    a = x.astype(BF16)
    r = x - a.astype(F32)
    b = r.astype(BF16)
    c = (r - b.astype(F32)).astype(BF16)
    return a, b, c


def first_kernel(g_hbm, e_hbm, s_hbm, c_ref, part_ref, g, e, s, sems):
    parts, _, step = part_ref.shape
    copies = [pltpu.make_async_copy(s_hbm, s, sems.at[0])]
    for k in range(parts):
        at = pl.ds(k * step, step)
        copies.append(pltpu.make_async_copy(g_hbm.at[at], g.at[at], sems.at[2 * k + 1]))
        copies.append(pltpu.make_async_copy(e_hbm.at[at], e.at[at], sems.at[2 * k + 2]))
    for copy in copies:
        copy.start()
    copies[0].wait()
    q = s[...].astype(BF16)
    for k in range(parts):
        copies[2 * k + 1].wait()
        copies[2 * k + 2].wait()
        at = pl.ds(k * step, step)
        c = (g[at].astype(F32) + e[at].astype(F32)).astype(BF16)
        c_ref[at] = c
        part_ref[k] = lax.dot_general(q, c, (((1,), (1,)), ((), ())), preferred_element_type=F32)


def first(g, e, s, parts):
    rows, cols = g.shape
    step = rows // parts
    return pl.pallas_call(
        first_kernel,
        in_specs=[pl.BlockSpec(memory_space=pltpu.HBM)] * 3,
        out_shape=[
            jax.ShapeDtypeStruct((rows, cols), BF16),
            jax.ShapeDtypeStruct((parts, RANK, step), F32),
        ],
        scratch_shapes=[
            VMEM((rows, cols), BF16),
            VMEM((rows, cols), BF16),
            VMEM((RANK, cols), F32),
            pltpu.SemaphoreType.DMA((2 * parts + 1,)),
        ],
        compiler_params=pltpu.CompilerParams(vmem_limit_bytes=16 << 20),
        name="first",
    )(*[pltpu.with_memory_space_constraint(x, pltpu.HBM) for x in (g, e, s)])


def sum_kernel(copies, x_ref, o_ref):
    total = x_ref[0]
    for k in range(1, x_ref.shape[0]):
        total = total + x_ref[k]
    for k in range(copies):
        o_ref[k] = total


def sum_copies(x, copies):
    return pl.pallas_call(
        functools.partial(sum_kernel, copies),
        out_shape=jax.ShapeDtypeStruct((copies,) + x.shape[1:], F32),
        compiler_params=pltpu.CompilerParams(vmem_limit_bytes=16 << 20),
        name="sum_copies",
    )(x)


def product_kernel(copies, p_ref, c_ref, o_ref):
    parts = p_ref.shape[0]
    terms = [split3(p_ref[k]) for k in range(parts)]
    left = jnp.concatenate([jnp.concatenate([t[j] for t in terms], axis=1) for j in range(3)], axis=0)
    t3 = jnp.dot(left, c_ref[...], preferred_element_type=F32)
    t = t3[:RANK] + t3[RANK : 2 * RANK] + t3[2 * RANK :]
    g3 = lax.dot_general(left, left, (((1,), (1,)), ((), ())), preferred_element_type=F32)
    gr = g3[:RANK] + g3[RANK : 2 * RANK] + g3[2 * RANK :]
    gram = gr[:, :RANK] + gr[:, RANK : 2 * RANK] + gr[:, 2 * RANK : 3 * RANK]
    packed = jnp.concatenate([gram[8 * k : 8 * k + 8] for k in range(4)], axis=1)
    chunks = c_ref.shape[1] // 128
    for k in range(copies):
        for j in range(chunks):
            o_ref[k, j * RANK : (j + 1) * RANK] = t[:, j * 128 : (j + 1) * 128]
        o_ref[k, chunks * RANK : chunks * RANK + 8] = packed


def product(p, c, copies):
    chunks = c.shape[1] // 128
    return pl.pallas_call(
        functools.partial(product_kernel, copies),
        out_shape=jax.ShapeDtypeStruct((copies, chunks * RANK + 8, 128), F32),
        compiler_params=pltpu.CompilerParams(vmem_limit_bytes=16 << 20),
        name="product",
    )(p, c)


def inverse_factor(gram, block=8):
    rows = lax.broadcasted_iota(jnp.int32, (RANK, 128), 0)
    cols = lax.broadcasted_iota(jnp.int32, (RANK, 128), 1)
    w = jnp.concatenate([gram, jnp.zeros((RANK, 128 - RANK), F32)], axis=1) + (rows + RANK == cols).astype(F32)
    pivot = jnp.ones((RANK, 128), F32)
    for first_col in range(0, RANK, block):
        wide = [jnp.broadcast_to(w[:, k : k + 1], (RANK, 128)) for k in range(first_col, first_col + block)]
        for j in range(block):
            k = first_col + j
            inv = 1.0 / wide[j][k : k + 1]
            pivot = jnp.where(rows == k, wide[j], pivot)
            col = jnp.where(rows > k, wide[j], 0.0) * inv
            for m in range(j + 1, block):
                wide[m] = wide[m] - col * wide[m][k : k + 1]
            w = w - col * w[k : k + 1]
    return (w / jnp.sqrt(pivot))[:, RANK : 2 * RANK]


def left_terms(x, axis):
    a, b, c = split3(x)
    return jnp.concatenate([a, a, b, a, b, c], axis=axis)


def right_terms(x):
    a, b, c = split3(x)
    return jnp.concatenate([a, b, a, c, b, a], axis=0)


def last_kernel(x_ref, p_ref, c_ref, comp_hbm, err_hbm, comp, err, sems):
    parts, _, step = p_ref.shape
    chunks = c_ref.shape[1] // 128
    total = x_ref[0]
    for k in range(1, x_ref.shape[0]):
        total = total + x_ref[k]
    packed = total[chunks * RANK :]
    gram = jnp.concatenate([packed[:, RANK * k : RANK * (k + 1)] for k in range(4)], axis=0)
    low = inverse_factor(gram)
    t = jnp.concatenate([total[j * RANK : (j + 1) * RANK] for j in range(chunks)], axis=1)
    inner = (((0,), (0,)), ((), ()))
    solve = lax.dot_general(left_terms(low, 0), right_terms(low), inner, preferred_element_type=F32)
    z = jnp.dot(left_terms(solve, 1), right_terms(t), preferred_element_type=F32)
    z1, z2, _ = split3(z)
    right = jnp.concatenate([z1, z2, z1], axis=0)
    copies = []
    for k in range(parts):
        p1, p2, _ = split3(p_ref[k])
        left = jnp.concatenate([p1, p1, p2], axis=0)
        rebuilt = lax.dot_general(left, right, inner, preferred_element_type=F32)
        at = pl.ds(k * step, step)
        comp[at] = rebuilt.astype(BF16)
        copies.append(pltpu.make_async_copy(comp.at[at], comp_hbm.at[at], sems.at[2 * k]))
        copies[-1].start()
        err[at] = (c_ref[at].astype(F32) - rebuilt).astype(BF16)
        copies.append(pltpu.make_async_copy(err.at[at], err_hbm.at[at], sems.at[2 * k + 1]))
        copies[-1].start()
    for copy in copies:
        copy.wait()


def last(x, p, c):
    return pl.pallas_call(
        last_kernel,
        out_specs=[pl.BlockSpec(memory_space=pltpu.HBM)] * 2,
        out_shape=[jax.ShapeDtypeStruct(c.shape, BF16)] * 2,
        scratch_shapes=[VMEM(c.shape, BF16), VMEM(c.shape, BF16), pltpu.SemaphoreType.DMA((2 * p.shape[0],))],
        compiler_params=pltpu.CompilerParams(vmem_limit_bytes=24 << 20),
        name="last",
    )(x, p, c)


def groups(size, key):
    table = {}
    for i in range(size):
        table.setdefault(key(i), []).append(i)
    return list(table.values())


def shards(near, far, plane, gradients, errors, start_factor):
    def exchange(x, axis, members):
        return lax.all_to_all(x, axis, 0, 0, tiled=True, axis_index_groups=members)

    parts = len(near[0])
    c, part = first(gradients[0], errors[0], start_factor[0], parts)
    part = exchange(part, "dp", near)
    piece = sum_copies(part, len(far[0]))
    piece = exchange(piece, "dp", far)
    piece = sum_copies(piece, parts)
    p = exchange(piece, "dp", near)
    t = product(p, c, len(plane[0][0]))
    t = exchange(t, ("dp", "fsdp"), plane[0])
    t = sum_copies(t, len(plane[1][0]))
    t = exchange(t, ("dp", "fsdp"), plane[1])
    compressed, new_errors = last(t, p, c)
    return compressed[None], new_errors[None]


def plane_groups(dp, fsdp, width, turn):
    def key(i):
        outer, inner = divmod(i, fsdp)
        if outer % 2 == turn:
            return outer, 0, inner // width
        return outer, 1, inner % width

    return groups(dp * fsdp, key)


def solution(mesh):
    dp, fsdp = mesh.shape["dp"], mesh.shape["fsdp"]
    body = functools.partial(
        shards,
        groups(dp, lambda i: i // 4),
        groups(dp, lambda i: i % 4),
        [plane_groups(dp, fsdp, 4, turn) for turn in range(2)],
    )
    return jax.shard_map(
        body,
        mesh=mesh,
        in_specs=(P(None, "fsdp", "dp"), P(None, "fsdp", "dp"), P(None, None, "dp")),
        out_specs=(P(None, "fsdp", "dp"), P(None, "fsdp", "dp")),
        check_vma=False,
    )
```

```python
import functools

import jax
import jax.numpy as jnp
from jax import lax
from jax.experimental import pallas as pl
from jax.experimental.pallas import tpu as pltpu
from jax.sharding import PartitionSpec as P

F32 = jnp.float32
LINE = [10, 11, 12, 13, 14, 15, 0, 1, 2, 3, 4, 5, 6, 7, 8, 9]
NEAR = [3, 2, 5, 1, 4, 7, 0, 6]
PLANE = [[2, 0, 1, 3], [2, 0, 1, 3]]
BF16 = jnp.bfloat16
RANK = 32
VMEM = pltpu.VMEM


def split3(x):
    a = x.astype(BF16)
    r = x - a.astype(F32)
    b = r.astype(BF16)
    c = (r - b.astype(F32)).astype(BF16)
    return a, b, c


def core_index():
    return lax.rem(lax.axis_index("dp"), 2)


def half_kernel(own, g_hbm, e_hbm, s_hbm, c_ref, part_ref, g, e, s, sems):
    parts, _, step = part_ref.shape
    half = core_index() if own else 1 - core_index()
    base = half * (parts * step)
    copies = [pltpu.make_async_copy(s_hbm, s, sems.at[0])]
    for k in range(parts):
        at, to = pl.ds(pl.multiple_of(base + k * step, step), step), pl.ds(k * step, step)
        copies.append(pltpu.make_async_copy(g_hbm.at[at], g.at[to], sems.at[2 * k + 1]))
        copies.append(pltpu.make_async_copy(e_hbm.at[at], e.at[to], sems.at[2 * k + 2]))
    for copy in copies:
        copy.start()
    copies[0].wait()
    q = s[...].astype(BF16)
    for k in range(parts):
        copies[2 * k + 1].wait()
        copies[2 * k + 2].wait()
        at = pl.ds(k * step, step)
        c = (g[at].astype(F32) + e[at].astype(F32)).astype(BF16)
        c_ref[at] = c
        part_ref[k] = lax.dot_general(q, c, (((1,), (1,)), ((), ())), preferred_element_type=F32)


def half_product(g, e, s, parts, own):
    rows, cols = g.shape
    rows //= 2
    step = rows // parts
    return pl.pallas_call(
        functools.partial(half_kernel, own),
        in_specs=[pl.BlockSpec(memory_space=pltpu.HBM)] * 3,
        out_shape=[
            jax.ShapeDtypeStruct((rows, cols), BF16),
            jax.ShapeDtypeStruct((parts, RANK, step), F32),
        ],
        scratch_shapes=[
            VMEM((rows, cols), BF16),
            VMEM((rows, cols), BF16),
            VMEM((RANK, cols), F32),
            pltpu.SemaphoreType.DMA((2 * parts + 1,)),
        ],
        compiler_params=pltpu.CompilerParams(vmem_limit_bytes=16 << 20),
        cost_estimate=pl.CostEstimate(flops=2 * RANK * rows * cols, bytes_accessed=6 * rows * cols, transcendentals=0),
        name="own_half" if own else "other_half",
    )(*[pltpu.with_memory_space_constraint(x, pltpu.HBM) for x in (g, e, s)])


def add_kernel(order, x_ref, y_ref, o_ref):
    for k in sorted(set(order)):
        total = x_ref[k] + y_ref[k]
        for j, piece in enumerate(order):
            if piece == k:
                o_ref[j] = total


def add_copies(x, y, order):
    return pl.pallas_call(
        functools.partial(add_kernel, order),
        out_shape=jax.ShapeDtypeStruct((len(order),) + x.shape[1:], F32),
        compiler_params=pltpu.CompilerParams(vmem_limit_bytes=16 << 20),
        name="add_copies",
    )(x, y)


def sum_kernel(copies, x_ref, o_ref):
    total = x_ref[0]
    for k in range(1, x_ref.shape[0]):
        total = total + x_ref[k]
    for k in range(copies):
        o_ref[k] = total


def sum_copies(x, copies):
    return pl.pallas_call(
        functools.partial(sum_kernel, copies),
        out_shape=jax.ShapeDtypeStruct((copies,) + x.shape[1:], F32),
        compiler_params=pltpu.CompilerParams(vmem_limit_bytes=16 << 20),
        name="sum_copies",
    )(x)


def take(p_ref, index, half):
    at = [NEAR.index(2 * index + core) for core in range(2)]
    return p_ref[at[0] + half * (at[1] - at[0])]


def row_blocks(p_ref, blocks):
    depth = p_ref.shape[0] // 2
    per = depth // blocks
    found = []
    for half in (core_index(), 1 - core_index()):
        for k in range(blocks):
            found.append(jnp.concatenate([take(p_ref, per * k + j, half) for j in range(per)], axis=0))
    return found


def product_kernel(copies, p_ref, own_ref, other_ref, o_ref):
    rows = own_ref.shape[0]
    terms = [split3(b) for b in row_blocks(p_ref, rows // 128)]
    left = jnp.concatenate([jnp.concatenate([t[j] for t in terms], axis=1) for j in range(3)], axis=0)
    t3 = jnp.dot(left[:, :rows], own_ref[...], preferred_element_type=F32)
    t3 = t3 + jnp.dot(left[:, rows:], other_ref[...], preferred_element_type=F32)
    t = t3[:RANK] + t3[RANK : 2 * RANK] + t3[2 * RANK :]
    g3 = lax.dot_general(left, left, (((1,), (1,)), ((), ())), preferred_element_type=F32)
    gr = g3[:RANK] + g3[RANK : 2 * RANK] + g3[2 * RANK :]
    gram = gr[:, :RANK] + gr[:, RANK : 2 * RANK] + gr[:, 2 * RANK : 3 * RANK]
    packed = jnp.concatenate([gram[8 * k : 8 * k + 8] for k in range(4)], axis=1)
    chunks = own_ref.shape[1] // 128
    for k in range(copies):
        for j in range(chunks):
            o_ref[k, j * RANK : (j + 1) * RANK] = t[:, j * 128 : (j + 1) * 128]
        o_ref[k, chunks * RANK : chunks * RANK + 8] = packed


def product(p, own, other, copies):
    return pl.pallas_call(
        functools.partial(product_kernel, copies),
        out_shape=jax.ShapeDtypeStruct((copies, own.shape[1] // 128 * RANK + 8, 128), F32),
        compiler_params=pltpu.CompilerParams(vmem_limit_bytes=16 << 20),
        name="product",
    )(p, own, other)


def inverse_factor(gram, block=16):
    rows = lax.broadcasted_iota(jnp.int32, (RANK, 128), 0)
    cols = lax.broadcasted_iota(jnp.int32, (RANK, 128), 1)
    w = jnp.concatenate([gram, jnp.zeros((RANK, 128 - RANK), F32)], axis=1) + (rows + RANK == cols).astype(F32)
    pivot = jnp.ones((RANK, 128), F32)
    for first_col in range(0, RANK, block):
        wide = [jnp.broadcast_to(w[:, k : k + 1], (RANK, 128)) for k in range(first_col, first_col + block)]
        for j in range(block):
            k = first_col + j
            inv = 1.0 / wide[j][k : k + 1]
            pivot = jnp.where(rows == k, wide[j], pivot)
            col = jnp.where(rows > k, wide[j], 0.0) * inv
            for m in range(j + 1, block):
                wide[m] = wide[m] - col * wide[m][k : k + 1]
            w = w - col * w[k : k + 1]
    return (w / jnp.sqrt(pivot))[:, RANK : 2 * RANK]


def left_terms(x, axis):
    a, b, c = split3(x)
    return jnp.concatenate([a, a, b, a, b, c], axis=axis)


def right_terms(x):
    a, b, c = split3(x)
    return jnp.concatenate([a, b, a, c, b, a], axis=0)


def last_kernel(x_ref, p_ref, own_ref, other_ref, comp_hbm, err_hbm, comp, err, sems):
    rows, cols = own_ref.shape
    chunks = cols // 128
    step = 128
    total = x_ref[0]
    for k in range(1, x_ref.shape[0]):
        total = total + x_ref[k]
    packed = total[chunks * RANK :]
    gram = jnp.concatenate([packed[:, RANK * k : RANK * (k + 1)] for k in range(4)], axis=0)
    low = inverse_factor(gram)
    t = jnp.concatenate([total[j * RANK : (j + 1) * RANK] for j in range(chunks)], axis=1)
    inner = (((0,), (0,)), ((), ()))
    solve = lax.dot_general(left_terms(low, 0), right_terms(low), inner, preferred_element_type=F32)
    z = jnp.dot(left_terms(solve, 1), right_terms(t), preferred_element_type=F32)
    z1, z2, _ = split3(z)
    right = jnp.concatenate([z1, z2, z1], axis=0)
    copies = []
    for k, block in enumerate(row_blocks(p_ref, rows // step)):
        p1, p2, _ = split3(block)
        left = jnp.concatenate([p1, p1, p2], axis=0)
        rebuilt = lax.dot_general(left, right, inner, preferred_element_type=F32)
        own = k < rows // step
        c_ref = own_ref if own else other_ref
        half = core_index() if own else 1 - core_index()
        inside = (k * step) % rows
        at = pl.ds(k * step, step)
        to = pl.ds(pl.multiple_of(half * rows + inside, step), step)
        comp[at] = rebuilt.astype(BF16)
        copies.append(pltpu.make_async_copy(comp.at[at], comp_hbm.at[to], sems.at[2 * k]))
        copies[-1].start()
        err[at] = (c_ref[pl.ds(inside, step)].astype(F32) - rebuilt).astype(BF16)
        copies.append(pltpu.make_async_copy(err.at[at], err_hbm.at[to], sems.at[2 * k + 1]))
        copies[-1].start()
    for copy in copies:
        copy.wait()


def last(x, p, own, other):
    rows, cols = own.shape
    whole = (2 * rows, cols)
    return pl.pallas_call(
        last_kernel,
        out_specs=[pl.BlockSpec(memory_space=pltpu.HBM)] * 2,
        out_shape=[jax.ShapeDtypeStruct(whole, BF16)] * 2,
        scratch_shapes=[VMEM(whole, BF16), VMEM(whole, BF16), pltpu.SemaphoreType.DMA((4 * rows // 128,))],
        compiler_params=pltpu.CompilerParams(vmem_limit_bytes=24 << 20),
        name="last",
    )(x, p, own, other)


def groups(size, key):
    table = {}
    for i in range(size):
        table.setdefault(key(i), []).append(i)
    return list(table.values())


def shards(swap, line, near, plane, gradients, errors, start_factor):
    def exchange(x, axis, members):
        return lax.all_to_all(x, axis, 0, 0, tiled=True, axis_index_groups=members)

    g, e, s = gradients[0], errors[0], start_factor[0]
    other, theirs = half_product(g, e, s, 2, False)
    theirs = lax.ppermute(theirs, "dp", swap)
    own, mine = half_product(g, e, s, 2, True)
    depth = len(near[0]) // 2
    order = [member // 2 % depth for member in line[0]]
    piece = add_copies(mine.reshape(depth, -1, 128), theirs.reshape(depth, -1, 128), order)
    piece = exchange(piece, "dp", line)
    p = exchange(sum_copies(piece, len(near[0])), "dp", near)
    t = product(p, own, other, len(plane[0][0]))
    t = exchange(t, ("dp", "fsdp"), plane[0])
    t = sum_copies(t, len(plane[1][0]))
    t = exchange(t, ("dp", "fsdp"), plane[1])
    compressed, new_errors = last(t, p, own, other)
    return compressed[None], new_errors[None]


def plane_groups(dp, fsdp, width, turn):
    def key(i):
        outer, inner = divmod(i, fsdp)
        if outer % 2 == turn:
            return outer, 0, inner // width
        return outer, 1, inner % width

    return [[members[j] for j in PLANE[turn]] for members in groups(dp * fsdp, key)]


def solution(mesh):
    dp, fsdp = mesh.shape["dp"], mesh.shape["fsdp"]
    body = functools.partial(
        shards,
        [(i, i ^ 1) for i in range(dp)],
        [[2 * z + core for z in LINE] for core in range(2)],
        [[first + member for member in NEAR] for first in range(0, dp, len(NEAR))],
        [plane_groups(dp, fsdp, 4, turn) for turn in range(2)],
    )
    placed = (P(None, "fsdp", "dp"), P(None, "fsdp", "dp"), P(None, None, "dp"))
    return jax.shard_map(body, mesh=mesh, in_specs=placed, out_specs=placed[:2], check_vma=False)
```

```python
import functools

import jax
import jax.numpy as jnp
from jax import lax
from jax.experimental import pallas as pl
from jax.experimental.pallas import tpu as pltpu
from jax.sharding import PartitionSpec as P

F32 = jnp.float32
LINE = [10, 0, 1, 2, 3, 4, 5, 6, 7, 8, 9, 11, 12, 13, 14, 15]
NEAR = [3, 2, 5, 1, 4, 7, 0, 6]
PLANE = [[2, 0, 1, 3], [2, 0, 1, 3]]
BF16 = jnp.bfloat16
RANK = 32
VMEM = pltpu.VMEM


def split3(x):
    a = x.astype(BF16)
    r = x - a.astype(F32)
    b = r.astype(BF16)
    c = (r - b.astype(F32)).astype(BF16)
    return a, b, c


def core_index():
    return lax.rem(lax.axis_index("dp"), 2)


def first_kernel(g_hbm, e_hbm, s_hbm, own_ref, other_ref, q_ref, part_ref, g, e, s, sems):
    parts, _, step = part_ref.shape
    rows = parts * step
    copies = [pltpu.make_async_copy(s_hbm, s, sems.at[0])]
    for k in range(2 * parts):
        half = 1 - core_index() if k < parts else core_index()
        at = pl.ds(pl.multiple_of(half * rows + k % parts * step, step), step)
        to = pl.ds(k * step, step)
        copies.append(pltpu.make_async_copy(g_hbm.at[at], g.at[to], sems.at[2 * k + 1]))
        copies.append(pltpu.make_async_copy(e_hbm.at[at], e.at[to], sems.at[2 * k + 2]))
    for copy in copies:
        copy.start()
    copies[0].wait()
    q = s[...].astype(BF16)
    q_ref[...] = q
    for k in range(2 * parts):
        copies[2 * k + 1].wait()
        copies[2 * k + 2].wait()
        at = pl.ds(k * step, step)
        c = (g[at].astype(F32) + e[at].astype(F32)).astype(BF16)
        to = pl.ds(k % parts * step, step)
        if k < parts:
            other_ref[to] = c
            part_ref[k] = lax.dot_general(q, c, (((1,), (1,)), ((), ())), preferred_element_type=F32)
        else:
            own_ref[to] = c


def first(g, e, s, parts):
    rows, cols = g.shape
    step = rows // (2 * parts)
    return pl.pallas_call(
        first_kernel,
        in_specs=[pl.BlockSpec(memory_space=pltpu.HBM)] * 3,
        out_shape=[
            jax.ShapeDtypeStruct((rows // 2, cols), BF16),
            jax.ShapeDtypeStruct((rows // 2, cols), BF16),
            jax.ShapeDtypeStruct((RANK, cols), BF16),
            jax.ShapeDtypeStruct((parts, RANK, step), F32),
        ],
        scratch_shapes=[
            VMEM((rows, cols), BF16),
            VMEM((rows, cols), BF16),
            VMEM((RANK, cols), F32),
            pltpu.SemaphoreType.DMA((4 * parts + 1,)),
        ],
        compiler_params=pltpu.CompilerParams(vmem_limit_bytes=16 << 20),
        name="first",
    )(*[pltpu.with_memory_space_constraint(x, pltpu.HBM) for x in (g, e, s)])


def own_kernel(q_ref, c_ref, part_ref):
    parts, _, step = part_ref.shape
    for k in range(parts):
        c = c_ref[pl.ds(k * step, step)]
        part_ref[k] = lax.dot_general(q_ref[...], c, (((1,), (1,)), ((), ())), preferred_element_type=F32)


def own_product(q, c, parts):
    rows, cols = c.shape
    return pl.pallas_call(
        own_kernel,
        out_shape=jax.ShapeDtypeStruct((parts, RANK, rows // parts), F32),
        compiler_params=pltpu.CompilerParams(vmem_limit_bytes=16 << 20),
        cost_estimate=pl.CostEstimate(flops=2 * RANK * rows * cols, bytes_accessed=2 * rows * cols, transcendentals=0),
        name="own_product",
    )(q, c)


def add_kernel(order, x_ref, y_ref, o_ref):
    for k in sorted(set(order)):
        total = x_ref[k] + y_ref[k]
        for j, piece in enumerate(order):
            if piece == k:
                o_ref[j] = total


def add_copies(x, y, order):
    return pl.pallas_call(
        functools.partial(add_kernel, order),
        out_shape=jax.ShapeDtypeStruct((len(order),) + x.shape[1:], F32),
        compiler_params=pltpu.CompilerParams(vmem_limit_bytes=16 << 20),
        name="add_copies",
    )(x, y)


def sum_kernel(copies, x_ref, o_ref):
    total = x_ref[0]
    for k in range(1, x_ref.shape[0]):
        total = total + x_ref[k]
    for k in range(copies):
        o_ref[k] = total


def sum_copies(x, copies):
    return pl.pallas_call(
        functools.partial(sum_kernel, copies),
        out_shape=jax.ShapeDtypeStruct((copies,) + x.shape[1:], F32),
        compiler_params=pltpu.CompilerParams(vmem_limit_bytes=16 << 20),
        name="sum_copies",
    )(x)


def take(p_ref, index, half):
    at = [NEAR.index(2 * index + core) for core in range(2)]
    return p_ref[at[0] + half * (at[1] - at[0])]


def row_blocks(p_ref, blocks):
    depth = p_ref.shape[0] // 2
    per = depth // blocks
    found = []
    for half in (core_index(), 1 - core_index()):
        for k in range(blocks):
            found.append(jnp.concatenate([take(p_ref, per * k + j, half) for j in range(per)], axis=0))
    return found


def product_kernel(copies, p_ref, own_ref, other_ref, o_ref):
    rows = own_ref.shape[0]
    terms = [split3(b) for b in row_blocks(p_ref, rows // 128)]
    left = jnp.concatenate([jnp.concatenate([t[j] for t in terms], axis=1) for j in range(3)], axis=0)
    t3 = jnp.dot(left[:, :rows], own_ref[...], preferred_element_type=F32)
    t3 = t3 + jnp.dot(left[:, rows:], other_ref[...], preferred_element_type=F32)
    t = t3[:RANK] + t3[RANK : 2 * RANK] + t3[2 * RANK :]
    g3 = lax.dot_general(left, left, (((1,), (1,)), ((), ())), preferred_element_type=F32)
    gr = g3[:RANK] + g3[RANK : 2 * RANK] + g3[2 * RANK :]
    gram = gr[:, :RANK] + gr[:, RANK : 2 * RANK] + gr[:, 2 * RANK : 3 * RANK]
    packed = jnp.concatenate([gram[8 * k : 8 * k + 8] for k in range(4)], axis=1)
    chunks = own_ref.shape[1] // 128
    for k in range(copies):
        for j in range(chunks):
            o_ref[k, j * RANK : (j + 1) * RANK] = t[:, j * 128 : (j + 1) * 128]
        o_ref[k, chunks * RANK : chunks * RANK + 8] = packed


def product(p, own, other, copies):
    return pl.pallas_call(
        functools.partial(product_kernel, copies),
        out_shape=jax.ShapeDtypeStruct((copies, own.shape[1] // 128 * RANK + 8, 128), F32),
        compiler_params=pltpu.CompilerParams(vmem_limit_bytes=16 << 20),
        name="product",
    )(p, own, other)


def inverse_factor(gram, block=16):
    rows = lax.broadcasted_iota(jnp.int32, (RANK, 128), 0)
    cols = lax.broadcasted_iota(jnp.int32, (RANK, 128), 1)
    w = jnp.concatenate([gram, jnp.zeros((RANK, 128 - RANK), F32)], axis=1) + (rows + RANK == cols).astype(F32)
    pivot = jnp.ones((RANK, 128), F32)
    for first_col in range(0, RANK, block):
        wide = [jnp.broadcast_to(w[:, k : k + 1], (RANK, 128)) for k in range(first_col, first_col + block)]
        for j in range(block):
            k = first_col + j
            inv = 1.0 / wide[j][k : k + 1]
            pivot = jnp.where(rows == k, wide[j], pivot)
            col = jnp.where(rows > k, wide[j], 0.0) * inv
            for m in range(j + 1, block):
                wide[m] = wide[m] - col * wide[m][k : k + 1]
            w = w - col * w[k : k + 1]
    return (w / jnp.sqrt(pivot))[:, RANK : 2 * RANK]


def left_terms(x, axis):
    a, b, c = split3(x)
    return jnp.concatenate([a, a, b, a, b, c], axis=axis)


def right_terms(x):
    a, b, c = split3(x)
    return jnp.concatenate([a, b, a, c, b, a], axis=0)


def last_kernel(x_ref, p_ref, own_ref, other_ref, comp_hbm, err_hbm, comp, err, sems):
    rows, cols = own_ref.shape
    chunks = cols // 128
    step = 128
    total = x_ref[0]
    for k in range(1, x_ref.shape[0]):
        total = total + x_ref[k]
    packed = total[chunks * RANK :]
    gram = jnp.concatenate([packed[:, RANK * k : RANK * (k + 1)] for k in range(4)], axis=0)
    low = inverse_factor(gram)
    t = jnp.concatenate([total[j * RANK : (j + 1) * RANK] for j in range(chunks)], axis=1)
    inner = (((0,), (0,)), ((), ()))
    solve = lax.dot_general(left_terms(low, 0), right_terms(low), inner, preferred_element_type=F32)
    z = jnp.dot(left_terms(solve, 1), right_terms(t), preferred_element_type=F32)
    z1, z2, _ = split3(z)
    right = jnp.concatenate([z1, z2, z1], axis=0)
    copies = []
    for k, block in enumerate(row_blocks(p_ref, rows // step)):
        p1, p2, _ = split3(block)
        left = jnp.concatenate([p1, p1, p2], axis=0)
        rebuilt = lax.dot_general(left, right, inner, preferred_element_type=F32)
        own = k < rows // step
        c_ref = own_ref if own else other_ref
        half = core_index() if own else 1 - core_index()
        inside = (k * step) % rows
        at = pl.ds(k * step, step)
        to = pl.ds(pl.multiple_of(half * rows + inside, step), step)
        comp[at] = rebuilt.astype(BF16)
        copies.append(pltpu.make_async_copy(comp.at[at], comp_hbm.at[to], sems.at[2 * k]))
        copies[-1].start()
        err[at] = (c_ref[pl.ds(inside, step)].astype(F32) - rebuilt).astype(BF16)
        copies.append(pltpu.make_async_copy(err.at[at], err_hbm.at[to], sems.at[2 * k + 1]))
        copies[-1].start()
    for copy in copies:
        copy.wait()


def last(x, p, own, other):
    rows, cols = own.shape
    whole = (2 * rows, cols)
    return pl.pallas_call(
        last_kernel,
        out_specs=[pl.BlockSpec(memory_space=pltpu.HBM)] * 2,
        out_shape=[jax.ShapeDtypeStruct(whole, BF16)] * 2,
        scratch_shapes=[VMEM(whole, BF16), VMEM(whole, BF16), pltpu.SemaphoreType.DMA((4 * rows // 128,))],
        compiler_params=pltpu.CompilerParams(vmem_limit_bytes=24 << 20),
        name="last",
    )(x, p, own, other)


def groups(size, key):
    table = {}
    for i in range(size):
        table.setdefault(key(i), []).append(i)
    return list(table.values())


def shards(swap, line, near, plane, gradients, errors, start_factor):
    def exchange(x, axis, members):
        return lax.all_to_all(x, axis, 0, 0, tiled=True, axis_index_groups=members)

    g, e, s = gradients[0], errors[0], start_factor[0]
    own, other, q, theirs = first(g, e, s, 2)
    theirs = lax.ppermute(theirs, "dp", swap)
    mine = own_product(q, own, 2)
    depth = len(near[0]) // 2
    order = [member // 2 % depth for member in line[0]]
    piece = add_copies(mine.reshape(depth, -1, 128), theirs.reshape(depth, -1, 128), order)
    piece = exchange(piece, "dp", line)
    p = exchange(sum_copies(piece, len(near[0])), "dp", near)
    t = product(p, own, other, len(plane[0][0]))
    t = exchange(t, ("dp", "fsdp"), plane[0])
    t = sum_copies(t, len(plane[1][0]))
    t = exchange(t, ("dp", "fsdp"), plane[1])
    compressed, new_errors = last(t, p, own, other)
    return compressed[None], new_errors[None]


def plane_groups(dp, fsdp, width, turn):
    def key(i):
        outer, inner = divmod(i, fsdp)
        if outer % 2 == turn:
            return outer, 0, inner // width
        return outer, 1, inner % width

    return [[members[j] for j in PLANE[turn]] for members in groups(dp * fsdp, key)]


def solution(mesh):
    dp, fsdp = mesh.shape["dp"], mesh.shape["fsdp"]
    body = functools.partial(
        shards,
        [(i, i ^ 1) for i in range(dp)],
        [[2 * z + core for z in LINE] for core in range(2)],
        [[first + member for member in NEAR] for first in range(0, dp, len(NEAR))],
        [plane_groups(dp, fsdp, 4, turn) for turn in range(2)],
    )
    placed = (P(None, "fsdp", "dp"), P(None, "fsdp", "dp"), P(None, None, "dp"))
    return jax.shard_map(body, mesh=mesh, in_specs=placed, out_specs=placed[:2], check_vma=False)
```

```python
import functools

import jax
import jax.numpy as jnp
from jax import lax
from jax.experimental import pallas as pl
from jax.experimental.pallas import tpu as pltpu
from jax.sharding import PartitionSpec as P

F32 = jnp.float32
LINE = [10, 0, 1, 2, 3, 4, 5, 6, 7, 8, 9, 11, 12, 13, 14, 15]
NEAR = [3, 2, 5, 1, 4, 7, 0, 6]
PLANE = [[2, 0, 1, 3], [2, 0, 1, 3]]
BF16 = jnp.bfloat16
LIFT = 2.0**60
RANK = 32
VMEM = pltpu.VMEM


def split3(x):
    a = x.astype(BF16)
    r = x - a.astype(F32)
    b = r.astype(BF16)
    c = (r - b.astype(F32)).astype(BF16)
    return a, b, c


def core_index():
    return lax.rem(lax.axis_index("dp"), 2)


def first_kernel(g_hbm, e_hbm, s_hbm, own_ref, other_ref, q_ref, part_ref, g, e, s, sems):
    parts, _, step = part_ref.shape
    rows = parts * step
    copies = [pltpu.make_async_copy(s_hbm, s, sems.at[0])]
    for k in range(2 * parts):
        half = 1 - core_index() if k < parts else core_index()
        at = pl.ds(pl.multiple_of(half * rows + k % parts * step, step), step)
        to = pl.ds(k * step, step)
        copies.append(pltpu.make_async_copy(g_hbm.at[at], g.at[to], sems.at[2 * k + 1]))
        copies.append(pltpu.make_async_copy(e_hbm.at[at], e.at[to], sems.at[2 * k + 2]))
    for copy in copies:
        copy.start()
    copies[0].wait()
    q = s[...].astype(BF16)
    q_ref[...] = q
    for k in range(2 * parts):
        copies[2 * k + 1].wait()
        copies[2 * k + 2].wait()
        at = pl.ds(k * step, step)
        c = (g[at].astype(F32) + e[at].astype(F32)).astype(BF16)
        to = pl.ds(k % parts * step, step)
        if k < parts:
            other_ref[to] = c
            part_ref[k] = lax.dot_general(q, c, (((1,), (1,)), ((), ())), preferred_element_type=F32)
        else:
            own_ref[to] = c


def first(g, e, s, parts):
    rows, cols = g.shape
    step = rows // (2 * parts)
    return pl.pallas_call(
        first_kernel,
        in_specs=[pl.BlockSpec(memory_space=pltpu.HBM)] * 3,
        out_shape=[
            jax.ShapeDtypeStruct((rows // 2, cols), BF16),
            jax.ShapeDtypeStruct((rows // 2, cols), BF16),
            jax.ShapeDtypeStruct((RANK, cols), BF16),
            jax.ShapeDtypeStruct((parts, RANK, step), F32),
        ],
        scratch_shapes=[
            VMEM((rows, cols), BF16),
            VMEM((rows, cols), BF16),
            VMEM((RANK, cols), F32),
            pltpu.SemaphoreType.DMA((4 * parts + 1,)),
        ],
        compiler_params=pltpu.CompilerParams(vmem_limit_bytes=16 << 20),
        name="first",
    )(*[pltpu.with_memory_space_constraint(x, pltpu.HBM) for x in (g, e, s)])


def own_kernel(q_ref, c_ref, part_ref):
    parts, _, step = part_ref.shape
    for k in range(parts):
        c = c_ref[pl.ds(k * step, step)]
        part_ref[k] = lax.dot_general(q_ref[...], c, (((1,), (1,)), ((), ())), preferred_element_type=F32)


def own_product(q, c, parts):
    rows, cols = c.shape
    return pl.pallas_call(
        own_kernel,
        out_shape=jax.ShapeDtypeStruct((parts, RANK, rows // parts), F32),
        compiler_params=pltpu.CompilerParams(vmem_limit_bytes=16 << 20),
        cost_estimate=pl.CostEstimate(flops=2 * RANK * rows * cols, bytes_accessed=2 * rows * cols, transcendentals=0),
        name="own_product",
    )(q, c)


def add_kernel(order, x_ref, y_ref, o_ref):
    for k in sorted(set(order)):
        total = x_ref[k] + y_ref[k]
        for j, piece in enumerate(order):
            if piece == k:
                o_ref[j] = total


def add_copies(x, y, order):
    return pl.pallas_call(
        functools.partial(add_kernel, order),
        out_shape=jax.ShapeDtypeStruct((len(order),) + x.shape[1:], F32),
        compiler_params=pltpu.CompilerParams(vmem_limit_bytes=16 << 20),
        name="add_copies",
    )(x, y)


def sum_kernel(copies, x_ref, o_ref):
    total = x_ref[0]
    for k in range(1, x_ref.shape[0]):
        total = total + x_ref[k]
    for k in range(copies):
        o_ref[k] = total


def sum_copies(x, copies):
    return pl.pallas_call(
        functools.partial(sum_kernel, copies),
        out_shape=jax.ShapeDtypeStruct((copies,) + x.shape[1:], F32),
        compiler_params=pltpu.CompilerParams(vmem_limit_bytes=16 << 20),
        name="sum_copies",
    )(x)


def take(p_ref, index, half):
    at = [NEAR.index(2 * index + core) for core in range(2)]
    return p_ref[at[0] + half * (at[1] - at[0])]


def row_blocks(p_ref, blocks):
    depth = p_ref.shape[0] // 2
    per = depth // blocks
    found = []
    for half in (core_index(), 1 - core_index()):
        for k in range(blocks):
            found.append(jnp.concatenate([take(p_ref, per * k + j, half) for j in range(per)], axis=0))
    return found


def product_kernel(copies, p_ref, own_ref, other_ref, o_ref):
    rows = own_ref.shape[0]
    terms = [split3(b) for b in row_blocks(p_ref, rows // 128)]
    left = jnp.concatenate([jnp.concatenate([t[j] for t in terms], axis=1) for j in range(3)], axis=0)
    lifted = left * jnp.asarray(LIFT, BF16)
    t3 = jnp.dot(lifted[:, :rows], own_ref[...], preferred_element_type=F32)
    t3 = t3 + jnp.dot(lifted[:, rows:], other_ref[...], preferred_element_type=F32)
    t = t3[:RANK] + t3[RANK : 2 * RANK] + t3[2 * RANK :]
    g3 = lax.dot_general(left, left, (((1,), (1,)), ((), ())), preferred_element_type=F32)
    gr = g3[:RANK] + g3[RANK : 2 * RANK] + g3[2 * RANK :]
    gram = gr[:, :RANK] + gr[:, RANK : 2 * RANK] + gr[:, 2 * RANK : 3 * RANK]
    packed = jnp.concatenate([gram[8 * k : 8 * k + 8] for k in range(4)], axis=1)
    chunks = own_ref.shape[1] // 128
    for k in range(copies):
        for j in range(chunks):
            o_ref[k, j * RANK : (j + 1) * RANK] = t[:, j * 128 : (j + 1) * 128]
        o_ref[k, chunks * RANK : chunks * RANK + 8] = packed


def product(p, own, other, copies):
    return pl.pallas_call(
        functools.partial(product_kernel, copies),
        out_shape=jax.ShapeDtypeStruct((copies, own.shape[1] // 128 * RANK + 8, 128), F32),
        compiler_params=pltpu.CompilerParams(vmem_limit_bytes=16 << 20),
        name="product",
    )(p, own, other)


def inverse_factor(gram, block=16):
    rows = lax.broadcasted_iota(jnp.int32, (RANK, 128), 0)
    cols = lax.broadcasted_iota(jnp.int32, (RANK, 128), 1)
    w = jnp.concatenate([gram, jnp.zeros((RANK, 128 - RANK), F32)], axis=1) + (rows + RANK == cols).astype(F32)
    pivot = jnp.ones((RANK, 128), F32)
    for first_col in range(0, RANK, block):
        wide = [jnp.broadcast_to(w[:, k : k + 1], (RANK, 128)) for k in range(first_col, first_col + block)]
        for j in range(block):
            k = first_col + j
            inv = 1.0 / wide[j][k : k + 1]
            pivot = jnp.where(rows == k, wide[j], pivot)
            col = jnp.where(rows > k, wide[j], 0.0) * inv
            for m in range(j + 1, block):
                wide[m] = wide[m] - col * wide[m][k : k + 1]
            w = w - col * w[k : k + 1]
    return (w / jnp.sqrt(pivot))[:, RANK : 2 * RANK]


def left_terms(x, axis):
    a, b, c = split3(x)
    return jnp.concatenate([a, a, b, a, b, c], axis=axis)


def right_terms(x):
    a, b, c = split3(x)
    return jnp.concatenate([a, b, a, c, b, a], axis=0)


def last_kernel(x_ref, p_ref, own_ref, other_ref, comp_hbm, err_hbm, comp, err, sems):
    rows, cols = own_ref.shape
    chunks = cols // 128
    step = 128
    total = x_ref[0]
    for k in range(1, x_ref.shape[0]):
        total = total + x_ref[k]
    packed = total[chunks * RANK :]
    gram = jnp.concatenate([packed[:, RANK * k : RANK * (k + 1)] for k in range(4)], axis=0)
    low = inverse_factor(gram)
    t = jnp.concatenate([total[j * RANK : (j + 1) * RANK] for j in range(chunks)], axis=1)
    inner = (((0,), (0,)), ((), ()))
    solve = lax.dot_general(left_terms(low, 0), right_terms(low), inner, preferred_element_type=F32)
    z = jnp.dot(left_terms(solve, 1), right_terms(t), preferred_element_type=F32)
    z1, z2, _ = split3(z * (1.0 / LIFT))
    right = jnp.concatenate([z1, z2, z1], axis=0)
    copies = []
    for k, block in enumerate(row_blocks(p_ref, rows // step)):
        p1, p2, _ = split3(block)
        left = jnp.concatenate([p1, p1, p2], axis=0)
        rebuilt = lax.dot_general(left, right, inner, preferred_element_type=F32)
        own = k < rows // step
        c_ref = own_ref if own else other_ref
        half = core_index() if own else 1 - core_index()
        inside = (k * step) % rows
        at = pl.ds(k * step, step)
        to = pl.ds(pl.multiple_of(half * rows + inside, step), step)
        comp[at] = rebuilt.astype(BF16)
        copies.append(pltpu.make_async_copy(comp.at[at], comp_hbm.at[to], sems.at[2 * k]))
        copies[-1].start()
        err[at] = (c_ref[pl.ds(inside, step)].astype(F32) - rebuilt).astype(BF16)
        copies.append(pltpu.make_async_copy(err.at[at], err_hbm.at[to], sems.at[2 * k + 1]))
        copies[-1].start()
    for copy in copies:
        copy.wait()


def last(x, p, own, other):
    rows, cols = own.shape
    whole = (2 * rows, cols)
    return pl.pallas_call(
        last_kernel,
        out_specs=[pl.BlockSpec(memory_space=pltpu.HBM)] * 2,
        out_shape=[jax.ShapeDtypeStruct(whole, BF16)] * 2,
        scratch_shapes=[VMEM(whole, BF16), VMEM(whole, BF16), pltpu.SemaphoreType.DMA((4 * rows // 128,))],
        compiler_params=pltpu.CompilerParams(vmem_limit_bytes=24 << 20),
        name="last",
    )(x, p, own, other)


def groups(size, key):
    table = {}
    for i in range(size):
        table.setdefault(key(i), []).append(i)
    return list(table.values())


def shards(swap, line, near, plane, gradients, errors, start_factor):
    def exchange(x, axis, members):
        return lax.all_to_all(x, axis, 0, 0, tiled=True, axis_index_groups=members)

    g, e, s = gradients[0], errors[0], start_factor[0]
    own, other, q, theirs = first(g, e, s, 2)
    theirs = lax.ppermute(theirs, "dp", swap)
    mine = own_product(q, own, 2)
    depth = len(near[0]) // 2
    order = [member // 2 % depth for member in line[0]]
    piece = add_copies(mine.reshape(depth, -1, 128), theirs.reshape(depth, -1, 128), order)
    piece = exchange(piece, "dp", line)
    p = exchange(sum_copies(piece, len(near[0])), "dp", near)
    t = product(p, own, other, len(plane[0][0]))
    t = exchange(t, ("dp", "fsdp"), plane[0])
    t = sum_copies(t, len(plane[1][0]))
    t = exchange(t, ("dp", "fsdp"), plane[1])
    compressed, new_errors = last(t, p, own, other)
    return compressed[None], new_errors[None]


def plane_groups(dp, fsdp, width, turn):
    def key(i):
        outer, inner = divmod(i, fsdp)
        if outer % 2 == turn:
            return outer, 0, inner // width
        return outer, 1, inner % width

    return [[members[j] for j in PLANE[turn]] for members in groups(dp * fsdp, key)]


def solution(mesh):
    dp, fsdp = mesh.shape["dp"], mesh.shape["fsdp"]
    body = functools.partial(
        shards,
        [(i, i ^ 1) for i in range(dp)],
        [[2 * z + core for z in LINE] for core in range(2)],
        [[first + member for member in NEAR] for first in range(0, dp, len(NEAR))],
        [plane_groups(dp, fsdp, 4, turn) for turn in range(2)],
    )
    placed = (P(None, "fsdp", "dp"), P(None, "fsdp", "dp"), P(None, None, "dp"))
    return jax.shard_map(body, mesh=mesh, in_specs=placed, out_specs=placed[:2], check_vma=False)
```
